32 devices in a mesh: row: 4 (over y, x), col: 8 (over z, core).
Axes of the slice: x: 2, y: 2, z: 4, core: 2. Of those that a mesh axis runs over, the one named last changes fastest.
Arguments:
- matrix: float32 [256, 40960], P('row', 'col'), as said below
- pivots: int32 [256], replicated, may hold values from 0 to 255, as said below
- check_weights: float32 [2, 256], P(None, 'row'), may hold values from -0.375 to 0.375
- checksum: float32 [2, 40960], P(None, 'col'), may hold values from -6 to 6
- coefficients: float32 [4, 8], P('row', 'col'), may hold values from 0.125 to 0.5
- checkpoints: int32 [4, 2], P('row'), may hold values from 0 to 3, as said below
Outputs:
- updated: float32 [256, 40960], P('row', 'col')
- new_checksum: float32 [2, 40960], P(None, 'col')
- parity: float32 [256, 40960], P('row', 'col')
The draws below stay inside these ranges and needn't reach their ends.
Inputs may be any that keep to these rules, and one draw needn't show every extreme that they name: `pivots`: 256 distinct row numbers. `checkpoints`: row index 0 keeps both codes on member 4 - 1, row index 1 on member 0. `matrix`: the first 256 columns are the panel's multipliers, of size about 256 ** -0.5.
All inputs are finite; a program needn't handle non-finite values.
Results may differ from the reference program's by a relative error of at most 0.000098.
Values sent between devices are 32-bit elements; how exact they have to be, the bound alone decides.
No kernel may reach another device: no remote copies, remote signals or barrier semaphores. Data moves between devices by JAX's collectives and lax.ppermute only.
A program may use at most 64 MiB of HBM per device.

```python
import math
import jax
import jax.numpy as jnp
from jax import lax

ORDER = 40960
NB = 256
CHK = 2
RB = 64
ROWS = 256
CB = 5120
GROUP = 4
N_ROW = 4
N_COL = 8


def draw_matrix(key, part):
    first = jax.random.fold_in(key, 0)
    values = jax.random.truncated_normal(first, -6.0, 6.0, (ROWS, ORDER), jnp.float32)
    column_ids = jnp.arange(ORDER)
    factor = jnp.where(column_ids < NB, NB ** (-0.5), 1.0).astype(jnp.float32)
    return values * factor[None, :]


def draw_pivots(key, part):
    return jax.random.permutation(key, ROWS)[:NB].astype(jnp.int32)


def draw_checkpoints(key, part):
    chosen = jax.random.randint(jax.random.fold_in(key, 7), (N_ROW, 2), 0, GROUP).astype(jnp.int32)
    row_ids = jnp.arange(N_ROW, dtype=jnp.int32)[:, None]
    chosen = jnp.where(row_ids == 0, jnp.int32(GROUP - 1), chosen)
    chosen = jnp.where(row_ids == 1, jnp.int32(0), chosen)
    return chosen.astype(jnp.int32)


def block_levels(rng, shape, pieces, low, largest):
    def one(axis_at, blocks):
        draws = jax.random.uniform(jax.random.fold_in(jax.random.fold_in(rng, 6), axis_at), (blocks,), jnp.float32, low / len(pieces), largest / len(pieces))
        return jnp.repeat(jnp.exp(draws), shape[axis_at] // blocks).reshape((-1,) + (1,) * (len(shape) - axis_at - 1))

    gain = one(*pieces[0])
    for cut in pieces[1:]:
        gain = gain * one(*cut)
    return gain


def gaussian(key, extent, scale, reach, shards=(), kind=jnp.bfloat16):
    level = block_levels(key, extent, shards, -0.22, 0.18) if shards else 1.0
    array = jax.random.normal(key, extent, jnp.float32) * scale * level
    return jnp.minimum(jnp.maximum(array, -reach), reach).astype(kind)


def setup_inputs(seed: int = 0) -> dict:
    keys = jax.random.split(jax.random.key(seed), 7)
    matrix = draw_matrix(jax.random.fold_in(keys[6], 71), 0)
    pivots = draw_pivots(jax.random.fold_in(keys[6], 71), 0)
    check_weights = gaussian(keys[2], (CHK, ROWS), ROWS ** -0.5, 0.375, ((1, 4),), jnp.float32)
    checksum = gaussian(keys[3], (CHK, ORDER), 1.0, 6.0, ((1, 8),), jnp.float32)
    coefficients = jnp.clip(jnp.exp(math.log(0.5) - 1.3862944 * jax.random.uniform(keys[4], (N_ROW, N_COL), jnp.float32) ** block_levels(keys[4], (N_ROW, N_COL), ((0, 4), (1, 8)), -0.2, 0.2)), 0.125, 0.5)
    checkpoints = draw_checkpoints(jax.random.fold_in(keys[6], 71), 0)
    return {"matrix": matrix, "pivots": pivots, "check_weights": check_weights, "checksum": checksum, "coefficients": coefficients, "checkpoints": checkpoints}


def reference(matrix, pivots, check_weights, checksum, coefficients, checkpoints):
    lower = matrix[:, :NB]
    picked = jnp.take(matrix, pivots.astype(jnp.int32), axis=0)
    column_ids = jnp.arange(ORDER, dtype=jnp.int32)
    upper = jnp.where(column_ids[None, :] >= NB, picked, jnp.float32(0.0))
    updated = matrix - jnp.dot(lower, upper, preferred_element_type=jnp.float32, precision=lax.Precision.HIGHEST)
    weighted_lower = jnp.dot(check_weights, lower, preferred_element_type=jnp.float32, precision=lax.Precision.HIGHEST)
    new_checksum = checksum - jnp.dot(weighted_lower, upper, preferred_element_type=jnp.float32, precision=lax.Precision.HIGHEST)
    weighted = matrix.reshape(N_ROW, RB, N_COL, CB) * coefficients[:, None, :, None]
    codes = jnp.sum(weighted.reshape(N_ROW, RB, GROUP, 2, CB), axis=2)
    spread = jnp.tile(codes, (1, 1, GROUP, 1))
    places = jnp.arange(N_COL, dtype=jnp.int32) // 2
    keepers = jnp.tile(checkpoints.astype(jnp.int32), (1, GROUP))
    member = places[None, :] == keepers
    parity = jnp.where(member[:, None, :, None], spread, jnp.float32(0.0)).reshape(ROWS, ORDER)
    return updated, new_checksum, parity
```

```python
import jax
import jax.numpy as jnp
from jax import lax
from jax.sharding import PartitionSpec as P

HIGHEST = lax.Precision.HIGHEST


def dot(a, b):
    return jnp.dot(a, b, preferred_element_type=jnp.float32, precision=HIGHEST)


def swap(value, axis, mask):
    route = [(i, i ^ mask) for i in range(lax.axis_size(axis))]
    return lax.ppermute(value, axis, route)


def hand_down(value, axis):
    index = lax.axis_index(axis)
    count = lax.axis_size(axis)
    step = count // 2
    while step:
        route = [(i, i + step) for i in range(0, count, 2 * step)]
        arrived = lax.ppermute(value, axis, route)
        value = jnp.where(index % (2 * step) == step, arrived, value)
        step //= 2
    return value


def span(bits):
    masks = [0]
    for bit in bits:
        masks += [mask | 1 << bit for mask in masks]
    return masks


def group_code(own, stride, position, count):
    bits = list(range(count.bit_length() - 1))
    piece = own
    for bit in bits[:-1]:
        half = piece.shape[0] // 2
        upper = position >> bit & 1 == 1
        first, second = piece[:half], piece[half:]
        arrived = swap(jnp.where(upper, first, second), "col", stride << bit)
        piece = jnp.where(upper, second, first) + arrived
    for bit in bits[-1:]:
        piece = piece + swap(piece, "col", stride << bit)
    for bit in reversed(bits[:-1]):
        upper = position >> bit & 1 == 1
        arrived = swap(piece, "col", stride << bit)
        piece = jnp.concatenate(
            [jnp.where(upper, arrived, piece), jnp.where(upper, piece, arrived)], axis=0
        )
    return piece


def per_device(matrix, pivots, check_weights, checksum, coefficients, checkpoints):
    rows, cols = matrix.shape
    width = pivots.shape[0]
    checks = check_weights.shape[0]
    row_index = lax.axis_index("row")
    col_index = lax.axis_index("col")
    n_row = lax.axis_size("row")
    n_col = lax.axis_size("col")
    groups = checkpoints.shape[1]

    bits = list(range(n_row.bit_length() - 1))
    cut = len(bits) // 2
    plans = [(bits[:cut], bits[cut:]), (bits[cut:], bits[:cut])]
    half = cols // 2

    gathered = []
    for number, (gather, _) in enumerate(plans):
        blocks = [matrix[:, number * half : (number + 1) * half]]
        for bit in gather:
            arrived = swap(jnp.concatenate(blocks, axis=0), "row", 1 << bit)
            blocks += [arrived[i * rows : (i + 1) * rows] for i in range(len(blocks))]
        gathered.append(jnp.concatenate(blocks, axis=0))

    lower = hand_down(jnp.where(col_index == 0, matrix[:, :width], jnp.float32(0.0)), "col")
    weighted = dot(check_weights, lower)
    weighted = jnp.pad(weighted, ((0, -checks % 8), (0, 0)))
    panel = {0: lower}
    total = weighted
    needed = set(span(plans[0][1])) | set(span(plans[1][1]))
    for mask in range(1, n_row):
        if mask in needed:
            arrived = swap(jnp.concatenate([lower, weighted], axis=0), "row", mask)
            panel[mask] = arrived[:rows]
            total = total + arrived[rows:]
        else:
            total = total + swap(weighted, "row", mask)

    outs = []
    sums = []
    for number, (gather, reduce) in enumerate(plans):
        places = [
            (row_index ^ mask) * rows + jnp.arange(rows, dtype=jnp.int32) for mask in span(gather)
        ]
        selector = (pivots[:, None] == jnp.concatenate(places)[None, :]).astype(jnp.float32)
        targets = span(reduce)
        left = dot(jnp.concatenate([panel[mask] for mask in targets] + [total], axis=0), selector)
        products = dot(left, gathered[number])
        part = {mask: products[i * rows : (i + 1) * rows] for i, mask in enumerate(targets)}
        check = products[len(targets) * rows :]
        for place in range(len(reduce) - 1, -1, -1):
            flip = 1 << reduce[place]
            keep = span(reduce[:place])
            message = jnp.concatenate([part[mask | flip] for mask in keep] + [check], axis=0)
            arrived = swap(message, "row", flip)
            part = {
                mask: part[mask] + arrived[i * rows : (i + 1) * rows]
                for i, mask in enumerate(keep)
            }
            check = check + arrived[len(keep) * rows :]
        live = col_index * cols + number * half + jnp.arange(half, dtype=jnp.int32) >= width
        there = slice(number * half, (number + 1) * half)
        outs.append(matrix[:, there] - jnp.where(live[None, :], part[0], jnp.float32(0.0)))
        sums.append(checksum[:, there] - jnp.where(live[None, :], check[:checks], jnp.float32(0.0)))
    updated = jnp.concatenate(outs, axis=1)
    new_checksum = jnp.concatenate(sums, axis=1)

    own = matrix * coefficients[0, 0]
    position = col_index // groups
    group_id = col_index % groups
    keeper = jnp.where(group_id == 0, checkpoints[0, 0], checkpoints[0, 1])
    members = n_col // groups
    pieces = []
    for low, high in ((0, rows // 4), (rows // 4, rows * 3 // 4), (rows * 3 // 4, rows)):
        pieces.append(group_code(own[low:high], groups, position, members))
    code = jnp.concatenate(pieces, axis=0)
    parity = jnp.where(position == keeper, code, jnp.float32(0.0))
    return (updated, new_checksum, parity)


def solution(mesh):
    in_specs = (
        P("row", "col"),
        P(),
        P(None, "row"),
        P(None, "col"),
        P("row", "col"),
        P("row", None),
    )
    out_specs = (P("row", "col"), P(None, "col"), P("row", "col"))
    return jax.shard_map(
        per_device, mesh=mesh, in_specs=in_specs, out_specs=out_specs, check_vma=False
    )
```

```python
import jax
import jax.numpy as jnp
from jax import lax
from jax.experimental import pallas as pl
from jax.experimental.pallas import tpu as pltpu
from jax.sharding import PartitionSpec as P


CUTS = (0, 1, 3, 4)
LANES = 128
GRANT = 8 << 20
ROOM = 67_043_328


VMEM = pl.BlockSpec(memory_space=pltpu.VMEM)
SMEM = pl.BlockSpec(memory_space=pltpu.SMEM)
HBM = pl.BlockSpec(memory_space=pltpu.HBM)


def near(value):
    return pltpu.with_memory_space_constraint(value, pltpu.VMEM)


def swap(value, axis, mask):
    return lax.ppermute(value, axis, [(i, i ^ mask) for i in range(lax.axis_size(axis))])


def span(bits):
    masks = [0]
    for bit in bits:
        masks += [mask | 1 << bit for mask in masks]
    return masks


def bits_of(count):
    return list(range(count.bit_length() - 1))


def plans_of(n_row):
    bits = bits_of(n_row)
    cut = len(bits) // 2
    return [(bits[:cut], bits[cut:]), (bits[cut:], bits[:cut])]


def panel_stages(n_col):
    bits = bits_of(n_col)[1:]
    stages = [bits[i : i + 2] for i in range(0, len(bits), 2)]
    return stages[::-1] + [[0]]


def call(
    kernel, shapes, in_specs, operands, scratch=(), places=None, aliases=None, flops=0, grant=GRANT
):
    places = places or [VMEM] * len(shapes)
    outs = [
        pltpu.VMEM(shape, jnp.float32) if place is VMEM else jax.ShapeDtypeStruct(shape, jnp.float32)
        for shape, place in zip(shapes, places)
    ]
    operands = [near(x) if spec is VMEM else x for x, spec in zip(operands, in_specs)]
    return pl.pallas_call(
        kernel,
        out_shape=outs,
        in_specs=in_specs,
        out_specs=places,
        scratch_shapes=list(scratch),
        input_output_aliases=aliases or {},
        compiler_params=pltpu.CompilerParams(vmem_limit_bytes=grant),
        cost_estimate=pl.CostEstimate(flops=flops, bytes_accessed=0, transcendentals=0),
    )(*operands)


def prepare(matrix, scale, groups, cuts, width):
    rows, cols = matrix.shape
    half = cols // 2
    sizes = [high - low for low, high in zip(cuts, cuts[1:])]

    def kernel(matrix_ref, scale_ref, *refs):
        sides, panel_ref, parts, sems = refs[:2], refs[2], refs[3:-1], refs[-1]
        copies = []
        for number, (low, high) in enumerate(zip(cuts, cuts[1:])):
            for side in range(2):
                copies.append(
                    pltpu.make_async_copy(
                        matrix_ref.at[low:high, side * half : (side + 1) * half],
                        sides[side].at[low:high, :],
                        sems.at[number, side],
                    )
                )
        for copy in copies:
            copy.start()
        scale = scale_ref[0, 0]
        upper = lax.axis_index("col") // groups & 1
        for number, (low, high) in enumerate(zip(cuts, cuts[1:])):
            size = (high - low) // 2
            for side in range(2):
                copies[2 * number + side].wait()
                there = slice(side * half, (side + 1) * half)
                for part in range(2):
                    other = 1 - upper if part == 0 else upper
                    start = pl.multiple_of(low + size * other, 8)
                    parts[2 * number + part][:, there] = (
                        sides[side][pl.ds(start, size), :] * scale
                    )
        panel_ref[...] = sides[0][:, :width]

    shapes = [(rows, half)] * 2 + [(rows, width)]
    for size in sizes:
        shapes += [(size // 2, cols)] * 2
    outs = call(
        kernel,
        shapes,
        [HBM, SMEM],
        [matrix, scale],
        scratch=[pltpu.SemaphoreType.DMA((len(sizes), 2))],
        grant=ROOM - 4 * (2 * rows * cols + rows * width) - (1 << 19),
    )
    parts = [(outs[3 + 2 * i], outs[4 + 2 * i]) for i in range(len(sizes))]
    return outs[:2], outs[2], parts


def choose(held, arrived, period, masks):
    def kernel(held_ref, *refs):
        digit = lax.axis_index("col") % period
        value = held_ref[...]
        for mask, ref in zip(masks, refs[:-1]):
            value = jnp.where(digit == mask, ref[...], value)
        refs[-1][...] = value

    specs = [VMEM] * (1 + len(arrived))
    return call(kernel, [held.shape], specs, [held, *arrived])[0]


def weigh(held, arrived, period, masks, check_weights):
    rows, width = held.shape
    checks = check_weights.shape[0]

    def kernel(weights_ref, held_ref, *refs):
        digit = lax.axis_index("col") % period
        value = held_ref[...]
        for mask, ref in zip(masks, refs[:-1]):
            value = jnp.where(digit == mask, ref[...], value)
        out_ref = refs[-1]
        out_ref[:rows] = value
        w1, w2, w3 = split(weights_ref[...], 3)
        p1, p2, p3 = split(value, 3)
        left = jnp.concatenate([w1, w1, w2, w2, w1, w3], axis=1)
        right = jnp.concatenate([p1, p2, p1, p2, p3, p1], axis=0)
        out_ref[rows:] = jnp.zeros((8, width), jnp.float32)
        out_ref[rows : rows + checks] = jnp.dot(left, right, preferred_element_type=jnp.float32)

    specs = [VMEM] * (2 + len(arrived))
    operands = [check_weights, held, *arrived]
    return call(kernel, [(rows + 8, width)], specs, operands)[0]


def fold(message, arrived):
    rows = message.shape[0] - 8

    def kernel(message_ref, *refs):
        refs[-1][:rows] = message_ref[:rows]
        total = message_ref[rows:]
        for ref in refs[:-1]:
            total = total + ref[rows:]
        refs[-1][rows:] = total

    return call(kernel, [message.shape], [VMEM] * (1 + len(arrived)), [message, *arrived])[0]


def add(a, b):
    def kernel(a_ref, b_ref, out_ref):
        out_ref[...] = a_ref[...] + b_ref[...]

    return call(kernel, [a.shape], [VMEM, VMEM], [a, b])[0]


def split(value, terms):
    pieces = []
    for _ in range(terms):
        piece = value.astype(jnp.bfloat16)
        value = value - piece.astype(jnp.float32)
        pieces.append(piece)
    return pieces


def multiply(masks, pivots, lefts, sums, blocks, checks):
    width = pivots.shape[1]
    rows, half = blocks[0].shape
    targets = len(lefts)
    depth = len(blocks) * rows
    step = half // max(1, half // 640)

    def kernel(pivots_ref, *refs):
        left_refs, refs = refs[:targets], refs[targets:]
        sum_refs, refs = refs[: len(sums)], refs[len(sums) :]
        block_refs, out_refs = refs[: len(blocks)], refs[len(blocks) :]
        row = lax.broadcasted_iota(jnp.int32, (rows, width), 0)
        own = lax.axis_index("row")
        selector = jnp.concatenate(
            [
                jnp.where(pivots_ref[...] == row + (own ^ mask) * rows, 1.0, 0.0)
                for mask in masks
            ],
            axis=0,
        ).astype(jnp.bfloat16)
        total = sum_refs[0][rows:]
        for ref in sum_refs[1:]:
            total = total + ref[rows:]
        stack = jnp.concatenate([ref[:rows] for ref in left_refs] + [total], axis=0)
        l1, l2 = [
            lax.dot_general(
                piece, selector, (((1,), (1,)), ((), ())), preferred_element_type=jnp.float32
            ).astype(jnp.bfloat16)
            for piece in split(stack, 2)
        ]
        left = jnp.concatenate([l1, l1, l2], axis=1)
        for out_ref in out_refs:
            out_ref[:, half:] = jnp.zeros((rows, LANES), jnp.float32)
        for low in range(0, half, step):
            there = slice(low, low + step)
            x1, x2 = split(jnp.concatenate([ref[:, there] for ref in block_refs], axis=0), 2)
            right = jnp.concatenate([x1, x2, x1], axis=0)
            product = jnp.dot(left, right, preferred_element_type=jnp.float32)
            for k, out_ref in enumerate(out_refs):
                out_ref[:, there] = product[k * rows : (k + 1) * rows]
                for at in range(0, step, LANES):
                    row = (low + at) // LANES * checks
                    out_ref[row : row + checks, half:] = product[
                        targets * rows : targets * rows + checks, at : at + LANES
                    ]

    return call(
        kernel,
        [(rows, half + LANES)] * targets,
        [VMEM] * (1 + targets + len(sums) + len(blocks)),
        [pivots, *lefts, *sums, *blocks],
        flops=2 * (targets * rows + 8) * depth * half,
    )


def subtract(number, matrix, checksum, width, kept, arrived, before):
    rows, half = matrix.shape
    checks, cols = checksum.shape
    pieces = 4

    def kernel(matrix_ref, checksum_ref, kept_ref, arrived_ref, *refs):
        updated_ref, sums_ref, block, line, sems = refs[-5:]
        there = slice(number * half, (number + 1) * half)
        lane = lax.broadcasted_iota(jnp.int32, (1, half), 1)
        live = lane + (lax.axis_index("col") * cols + number * half) >= width
        copies = []
        for k in range(pieces):
            low, high = k * rows // pieces, (k + 1) * rows // pieces
            product = kept_ref[low:high, :half] + arrived_ref[low:high, :half]
            block[low:high, :] = matrix_ref[low:high, :] - jnp.where(live, product, 0.0)
            copies.append(
                pltpu.make_async_copy(
                    block.at[low:high, :], updated_ref.at[low:high, there], sems.at[k]
                )
            )
            copies[-1].start()
        total = kept_ref[:, half:] + arrived_ref[:, half:]
        for at in range(0, half, LANES):
            row = at // LANES * checks
            line[:, at : at + LANES] = checksum_ref[
                :, number * half + at : number * half + at + LANES
            ] - jnp.where(live[:, at : at + LANES], total[row : row + checks], 0.0)
        copies.append(pltpu.make_async_copy(line, sums_ref.at[:, there], sems.at[pieces]))
        copies[-1].start()
        for copy in copies:
            copy.wait()

    return call(
        kernel,
        [(rows, cols), (checks, cols)],
        [VMEM] * 4 + [HBM] * len(before),
        [matrix, checksum, kept, arrived, *before],
        scratch=[
            pltpu.VMEM((rows, half), jnp.float32),
            pltpu.VMEM((checks, half), jnp.float32),
            pltpu.SemaphoreType.DMA((pieces + 1,)),
        ],
        places=[HBM, HBM],
        aliases={4 + i: i for i in range(len(before))},
    )


def store_code(checkpoints, low, piece, arrived, shape, before):
    size, cols = piece.shape
    groups = checkpoints.shape[1]

    def kernel(points_ref, piece_ref, arrived_ref, *refs):
        out_ref, block, sems = refs[-3:]
        index = lax.axis_index("col")
        position = index // groups
        keeper = points_ref[0, 0]
        for k in range(1, groups):
            keeper = jnp.where(index % groups == k, points_ref[0, k], keeper)
        keep = position == keeper
        upper = position & 1 == 1
        copies = []
        for k in range(2):
            there = slice(k * size, (k + 1) * size)
            mine = upper if k else jnp.logical_not(upper)
            value = jnp.where(mine, piece_ref[...], arrived_ref[...])
            block[there, :] = jnp.where(keep, value, 0.0)
            copies.append(
                pltpu.make_async_copy(
                    block.at[there, :],
                    out_ref.at[low + k * size : low + (k + 1) * size, :],
                    sems.at[k],
                )
            )
            copies[-1].start()
        for copy in copies:
            copy.wait()

    return call(
        kernel,
        [shape],
        [SMEM] + [VMEM] * 2 + [HBM] * len(before),
        [checkpoints, piece, arrived, *before],
        scratch=[
            pltpu.VMEM((2 * size, cols), jnp.float32),
            pltpu.SemaphoreType.DMA((2,)),
        ],
        places=[HBM],
        aliases={3 + i: i for i in range(len(before))},
    )


def halves(own, upper):
    half = own.shape[0] // 2
    first, second = own[:half], own[half:]
    return jnp.where(upper, first, second), jnp.where(upper, second, first)


def group_code(outgoing, kept, stride, position, count):
    bits = bits_of(count)
    for bit in bits[:-1]:
        arrived = swap(outgoing, "col", stride << bit)
        piece = add(kept, arrived)
        if bit + 2 < len(bits):
            outgoing, kept = halves(piece, position >> (bit + 1) & 1 == 1)
    for bit in bits[-1:]:
        arrived = swap(piece, "col", stride << bit)
        piece = add(piece, arrived)
    for bit in reversed(bits[:-1]):
        arrived = swap(piece, "col", stride << bit)
        if bit == 0:
            return piece, arrived
        upper = position >> bit & 1 == 1
        piece = jnp.concatenate(
            [jnp.where(upper, arrived, piece), jnp.where(upper, piece, arrived)], axis=0
        )


def per_device(matrix, pivots, check_weights, checksum, coefficients, checkpoints):
    rows, cols = matrix.shape
    width = pivots.shape[0]
    checks = check_weights.shape[0]
    col_index = lax.axis_index("col")
    n_row = lax.axis_size("row")
    n_col = lax.axis_size("col")
    groups = checkpoints.shape[1]
    plans = plans_of(n_row)

    position = col_index // groups
    cuts = [cut * rows // CUTS[-1] for cut in CUTS]
    sides, lower, parts = prepare(matrix, coefficients, groups, cuts, width)

    gathered = []
    for number, (gather, _) in enumerate(plans):
        blocks = [sides[number]]
        for bit in gather:
            message = blocks[0] if len(blocks) == 1 else jnp.concatenate(blocks, axis=0)
            arrived = swap(message, "row", 1 << bit)
            if len(blocks) == 1:
                blocks.append(arrived)
            else:
                blocks += [arrived[i * rows : (i + 1) * rows] for i in range(len(blocks))]
        gathered.append(blocks)

    stages = panel_stages(n_col)
    for number, bits in enumerate(stages):
        masks = span(bits)[1:]
        period = 1 << min(bits) + len(bits)
        came = []
        for mask in masks:
            route = [(i, i | mask) for i in range(0, n_col, period)]
            came.append(lax.ppermute(lower, "col", route))
        if number < len(stages) - 1:
            lower = choose(lower, came, period, masks)
        else:
            message = weigh(lower, came, period, masks, check_weights)
    panel = {}
    came = []
    for mask in span(plans[1][1])[1:]:
        panel[mask] = swap(message, "row", mask)
        came.append(panel[mask])
    message = fold(message, came)
    panel[0] = message
    sums = [message]
    for mask in span(plans[0][1])[1:]:
        panel[mask] = swap(message, "row", mask)
        sums.append(panel[mask])

    results = ()
    for number, (gather, reduce) in enumerate(plans):
        targets = span(reduce)
        lefts = [panel[mask] for mask in targets]
        outs = multiply(span(gather), pivots[None, :], lefts, sums, gathered[number], checks)
        part = dict(zip(targets, outs))
        for place in range(len(reduce) - 1, -1, -1):
            flip = 1 << reduce[place]
            keep = span(reduce[:place])
            sent = [part[mask | flip] for mask in keep]
            message = sent[0] if len(sent) == 1 else jnp.concatenate(sent, axis=0)
            arrived = swap(message, "row", flip)
            if place:
                part = {
                    mask: part[mask] + arrived[i * rows : (i + 1) * rows]
                    for i, mask in enumerate(keep)
                }
        results = subtract(
            number, sides[number], checksum, width, part[0], arrived, results
        )

    parity = ()
    for chunk, (outgoing, kept) in enumerate(parts):
        piece, arrived = group_code(outgoing, kept, groups, position, n_col // groups)
        parity = store_code(checkpoints, cuts[chunk], piece, arrived, (rows, cols), parity)
    return (*results, *parity)


def solution(mesh):
    in_specs = (
        P("row", "col"),
        P(),
        P(None, "row"),
        P(None, "col"),
        P("row", "col"),
        P("row", None),
    )
    out_specs = (P("row", "col"), P(None, "col"), P("row", "col"))
    return jax.shard_map(
        per_device, mesh=mesh, in_specs=in_specs, out_specs=out_specs, check_vma=False
    )
```

```python
import jax
import jax.numpy as jnp
from jax import lax
from jax.experimental import pallas as pl
from jax.experimental.pallas import tpu as pltpu
from jax.sharding import PartitionSpec as P


CUTS = (0, 8, 20, 32, 40)
LANES = 128
GRANT = 8 << 20
ROOM = 67_043_328


VMEM = pl.BlockSpec(memory_space=pltpu.VMEM)
SMEM = pl.BlockSpec(memory_space=pltpu.SMEM)
HBM = pl.BlockSpec(memory_space=pltpu.HBM)


def near(value):
    return pltpu.with_memory_space_constraint(value, pltpu.VMEM)


def swap(value, axis, mask):
    return lax.ppermute(value, axis, [(i, i ^ mask) for i in range(lax.axis_size(axis))])


def span(bits):
    masks = [0]
    for bit in bits:
        masks += [mask | 1 << bit for mask in masks]
    return masks


def bits_of(count):
    return list(range(count.bit_length() - 1))


def plans_of(n_row):
    bits = bits_of(n_row)
    cut = len(bits) // 2
    return [(bits[:cut], bits[cut:]), (bits[cut:], bits[:cut])]


def panel_stages(n_col):
    bits = bits_of(n_col)[1:]
    stages = [bits[i : i + 2] for i in range(0, len(bits), 2)]
    return stages[::-1] + [[0]]


def call(
    kernel, shapes, in_specs, operands, scratch=(), places=None, aliases=None, flops=0, grant=GRANT
):
    places = places or [VMEM] * len(shapes)
    outs = [
        pltpu.VMEM(shape, jnp.float32) if place is VMEM else jax.ShapeDtypeStruct(shape, jnp.float32)
        for shape, place in zip(shapes, places)
    ]
    operands = [near(x) if spec is VMEM else x for x, spec in zip(operands, in_specs)]
    return pl.pallas_call(
        kernel,
        out_shape=outs,
        in_specs=in_specs,
        out_specs=places,
        scratch_shapes=list(scratch),
        input_output_aliases=aliases or {},
        compiler_params=pltpu.CompilerParams(vmem_limit_bytes=grant),
        cost_estimate=pl.CostEstimate(flops=flops, bytes_accessed=0, transcendentals=0),
    )(*operands)


def prepare(matrix, scale, groups, cuts, width, carry):
    rows, cols = matrix.shape
    half = cols // 2
    deep = rows // 2
    count = len(cuts) - 1
    pieces = 2
    step = deep // pieces

    def kernel(matrix_ref, scale_ref, *refs):
        sides, panel_ref, parts, sems = refs[:2], refs[2], refs[3:-1], refs[-1]
        copies = []
        for piece in range(2 * pieces):
            lines = slice(piece * step, (piece + 1) * step)
            for side in range(2):
                copies.append(
                    pltpu.make_async_copy(
                        matrix_ref.at[lines, side * half : (side + 1) * half],
                        sides[side].at[lines, :],
                        sems.at[piece, side],
                    )
                )
        for copy in copies:
            copy.start()
        scale = scale_ref[0, 0]
        upper = lax.axis_index("col") // groups & 1
        for copy in copies:
            copy.wait()
        for number in range(count):
            for side in range(2):
                low = max(cuts[number], side * half)
                high = min(cuts[number + 1], (side + 1) * half)
                if low < high:
                    here = slice(low - side * half, high - side * half)
                    there = slice(low - cuts[number], high - cuts[number])
                    for part in range(2):
                        other = 1 - upper if part == 0 else upper
                        start = pl.multiple_of(deep * other, 8)
                        parts[2 * number + part][:, there] = (
                            sides[side][pl.ds(start, deep), here] * scale
                        )
        panel_ref[...] = sides[0][:, :width]
        if carry:
            for k in range(2):
                there = slice(cuts[1] + k * width, cuts[1] + (k + 1) * width)
                parts[0][:, there] = sides[0][k * deep : (k + 1) * deep, :width]

    shapes = [(rows, half)] * 2 + [(rows, width)]
    for number in range(count):
        size = cuts[number + 1] - cuts[number]
        shapes += [(deep, size + (2 * width if carry and number == 0 else 0)), (deep, size)]
    outs = call(
        kernel,
        shapes,
        [HBM, SMEM],
        [matrix, scale],
        scratch=[pltpu.SemaphoreType.DMA((2 * pieces, 2))],
        grant=ROOM - 4 * (2 * rows * cols + 2 * rows * width) - (1 << 19),
    )
    parts = [(outs[3 + 2 * i], outs[4 + 2 * i]) for i in range(count)]
    return outs[:2], outs[2], parts


def choose(held, arrived, field, masks):
    def kernel(held_ref, *refs):
        digit = lax.axis_index("col") & field
        value = held_ref[...]
        for mask, ref in zip(masks, refs[:-1]):
            value = jnp.where(digit == mask, ref[...], value)
        refs[-1][...] = value

    specs = [VMEM] * (1 + len(arrived))
    return call(kernel, [held.shape], specs, [held, *arrived])[0]


def weigh(held, arrived, field, masks, check_weights):
    rows, width = held.shape
    checks = check_weights.shape[0]

    def kernel(weights_ref, held_ref, *refs):
        digit = lax.axis_index("col") & field
        value = held_ref[...]
        for mask, ref in zip(masks, refs[:-1]):
            value = jnp.where(digit == mask, ref[...], value)
        out_ref = refs[-1]
        out_ref[:rows] = value
        w1, w2, w3 = split(weights_ref[...], 3)
        p1, p2, p3 = split(value, 3)
        left = jnp.concatenate([w1, w1, w2, w2, w1, w3], axis=1)
        right = jnp.concatenate([p1, p2, p1, p2, p3, p1], axis=0)
        out_ref[rows:] = jnp.zeros((8, width), jnp.float32)
        out_ref[rows : rows + checks] = jnp.dot(left, right, preferred_element_type=jnp.float32)

    specs = [VMEM] * (2 + len(arrived))
    operands = [check_weights, held, *arrived]
    return call(kernel, [(rows + 8, width)], specs, operands)[0]


def fold(message, arrived):
    rows = message.shape[0] - 8

    def kernel(message_ref, *refs):
        refs[-1][:rows] = message_ref[:rows]
        total = message_ref[rows:]
        for ref in refs[:-1]:
            total = total + ref[rows:]
        refs[-1][rows:] = total

    return call(kernel, [message.shape], [VMEM] * (1 + len(arrived)), [message, *arrived])[0]


def add(a, b):
    def kernel(a_ref, b_ref, out_ref):
        out_ref[...] = a_ref[...] + b_ref[...]

    return call(kernel, [a.shape], [VMEM, VMEM], [a, b])[0]


def add_and_unpack(kept, arrived, panel, groups):
    height, cols = kept.shape
    rows, width = panel.shape

    def kernel(kept_ref, arrived_ref, held_ref, out_ref, panel_ref):
        out_ref[...] = kept_ref[...] + arrived_ref[:, :cols]
        came = lax.axis_index("col") // groups & 1 == 1
        for k in range(rows // height):
            lines = slice(k * height, (k + 1) * height)
            there = slice(cols + k * width, cols + (k + 1) * width)
            panel_ref[lines, :] = jnp.where(came, arrived_ref[:, there], held_ref[lines, :])

    shapes = [kept.shape, panel.shape]
    return call(kernel, shapes, [VMEM] * 3, [kept, arrived, panel])


def split(value, terms):
    pieces = []
    for _ in range(terms):
        piece = value.astype(jnp.bfloat16)
        value = value - piece.astype(jnp.float32)
        pieces.append(piece)
    return pieces


def multiply(masks, pivots, lefts, sums, blocks, checks):
    width = pivots.shape[1]
    rows, half = blocks[0].shape
    targets = len(lefts)
    depth = len(blocks) * rows
    step = half // max(1, half // 640)

    def kernel(pivots_ref, *refs):
        left_refs, refs = refs[:targets], refs[targets:]
        sum_refs, refs = refs[: len(sums)], refs[len(sums) :]
        block_refs, out_refs = refs[: len(blocks)], refs[len(blocks) :]
        row = lax.broadcasted_iota(jnp.int32, (rows, width), 0)
        own = lax.axis_index("row")
        selector = jnp.concatenate(
            [
                jnp.where(pivots_ref[...] == row + (own ^ mask) * rows, 1.0, 0.0)
                for mask in masks
            ],
            axis=0,
        ).astype(jnp.bfloat16)
        total = sum_refs[0][rows:]
        for ref in sum_refs[1:]:
            total = total + ref[rows:]
        stack = jnp.concatenate([ref[:rows] for ref in left_refs] + [total], axis=0)
        l1, l2 = [
            lax.dot_general(
                piece, selector, (((1,), (1,)), ((), ())), preferred_element_type=jnp.float32
            ).astype(jnp.bfloat16)
            for piece in split(stack, 2)
        ]
        left = jnp.concatenate([l1, l1, l2], axis=1)
        for out_ref in out_refs:
            out_ref[:, half:] = jnp.zeros((rows, LANES), jnp.float32)
        for low in range(0, half, step):
            there = slice(low, low + step)
            x1, x2 = split(jnp.concatenate([ref[:, there] for ref in block_refs], axis=0), 2)
            right = jnp.concatenate([x1, x2, x1], axis=0)
            product = jnp.dot(left, right, preferred_element_type=jnp.float32)
            for k, out_ref in enumerate(out_refs):
                out_ref[:, there] = product[k * rows : (k + 1) * rows]
                for at in range(0, step, LANES):
                    row = (low + at) // LANES * checks
                    out_ref[row : row + checks, half:] = product[
                        targets * rows : targets * rows + checks, at : at + LANES
                    ]

    return call(
        kernel,
        [(rows, half + LANES)] * targets,
        [VMEM] * (1 + targets + len(sums) + len(blocks)),
        [pivots, *lefts, *sums, *blocks],
        flops=2 * (targets * rows + 8) * depth * half,
    )


def subtract(number, matrix, checksum, width, kept, arrived, before):
    rows, half = matrix.shape
    checks, cols = checksum.shape
    pieces = 4

    def kernel(matrix_ref, checksum_ref, kept_ref, arrived_ref, *refs):
        updated_ref, sums_ref, block, line, sems = refs[-5:]
        there = slice(number * half, (number + 1) * half)
        lane = lax.broadcasted_iota(jnp.int32, (1, half), 1)
        live = lane + (lax.axis_index("col") * cols + number * half) >= width
        copies = []
        for k in range(pieces):
            low, high = k * rows // pieces, (k + 1) * rows // pieces
            product = kept_ref[low:high, :half] + arrived_ref[low:high, :half]
            block[low:high, :] = matrix_ref[low:high, :] - jnp.where(live, product, 0.0)
            copies.append(
                pltpu.make_async_copy(
                    block.at[low:high, :], updated_ref.at[low:high, there], sems.at[k]
                )
            )
            copies[-1].start()
        total = kept_ref[:, half:] + arrived_ref[:, half:]
        for at in range(0, half, LANES):
            row = at // LANES * checks
            line[:, at : at + LANES] = checksum_ref[
                :, number * half + at : number * half + at + LANES
            ] - jnp.where(live[:, at : at + LANES], total[row : row + checks], 0.0)
        copies.append(pltpu.make_async_copy(line, sums_ref.at[:, there], sems.at[pieces]))
        copies[-1].start()
        for copy in copies:
            copy.wait()

    return call(
        kernel,
        [(rows, cols), (checks, cols)],
        [VMEM] * 4 + [HBM] * len(before),
        [matrix, checksum, kept, arrived, *before],
        scratch=[
            pltpu.VMEM((rows, half), jnp.float32),
            pltpu.VMEM((checks, half), jnp.float32),
            pltpu.SemaphoreType.DMA((pieces + 1,)),
        ],
        places=[HBM, HBM],
        aliases={4 + i: i for i in range(len(before))},
    )


def store_code(checkpoints, low, piece, arrived, shape, before):
    size, cols = piece.shape
    groups = checkpoints.shape[1]

    def kernel(points_ref, piece_ref, arrived_ref, *refs):
        out_ref, block, sems = refs[-3:]
        index = lax.axis_index("col")
        position = index // groups
        keeper = points_ref[0, 0]
        for k in range(1, groups):
            keeper = jnp.where(index % groups == k, points_ref[0, k], keeper)
        keep = position == keeper
        upper = position & 1 == 1
        copies = []
        for k in range(2):
            there = slice(k * size, (k + 1) * size)
            mine = upper if k else jnp.logical_not(upper)
            value = jnp.where(mine, piece_ref[...], arrived_ref[...])
            block[there, :] = jnp.where(keep, value, 0.0)
            copies.append(
                pltpu.make_async_copy(
                    block.at[there, :],
                    out_ref.at[there, low : low + cols],
                    sems.at[k],
                )
            )
            copies[-1].start()
        for copy in copies:
            copy.wait()

    return call(
        kernel,
        [shape],
        [SMEM] + [VMEM] * 2 + [HBM] * len(before),
        [checkpoints, piece, arrived, *before],
        scratch=[
            pltpu.VMEM((2 * size, cols), jnp.float32),
            pltpu.SemaphoreType.DMA((2,)),
        ],
        places=[HBM],
        aliases={3 + i: i for i in range(len(before))},
    )


def halves(own, upper):
    half = own.shape[0] // 2
    first, second = own[:half], own[half:]
    return jnp.where(upper, first, second), jnp.where(upper, second, first)


def reduce_code(outgoing, kept, stride, position, count):
    bits = bits_of(count)
    for bit in bits[:-1]:
        arrived = swap(outgoing, "col", stride << bit)
        piece = add(kept, arrived)
        if bit + 2 < len(bits):
            outgoing, kept = halves(piece, position >> (bit + 1) & 1 == 1)
    for bit in bits[-1:]:
        arrived = swap(piece, "col", stride << bit)
        piece = add(piece, arrived)
    return piece


def gather_code(piece, stride, position, count):
    bits = bits_of(count)
    for bit in reversed(bits[:-1]):
        arrived = swap(piece, "col", stride << bit)
        if bit == 0:
            return piece, arrived
        upper = position >> bit & 1 == 1
        piece = jnp.concatenate(
            [jnp.where(upper, arrived, piece), jnp.where(upper, piece, arrived)], axis=0
        )


def per_device(matrix, pivots, check_weights, checksum, coefficients, checkpoints):
    rows, cols = matrix.shape
    width = pivots.shape[0]
    checks = check_weights.shape[0]
    col_index = lax.axis_index("col")
    n_row = lax.axis_size("row")
    n_col = lax.axis_size("col")
    groups = checkpoints.shape[1]
    plans = plans_of(n_row)

    position = col_index // groups
    cuts = [cut * (cols // LANES) // CUTS[-1] * LANES for cut in CUTS]
    members = n_col // groups
    carry = len(bits_of(members)) == 2 and groups == 2
    sides, lower, parts = prepare(matrix, coefficients, groups, cuts, width, carry)

    gathered = []
    for number, (gather, _) in enumerate(plans):
        blocks = [sides[number]]
        for bit in gather:
            message = blocks[0] if len(blocks) == 1 else jnp.concatenate(blocks, axis=0)
            arrived = swap(message, "row", 1 << bit)
            if len(blocks) == 1:
                blocks.append(arrived)
            else:
                blocks += [arrived[i * rows : (i + 1) * rows] for i in range(len(blocks))]
        gathered.append(blocks)

    codes = []
    stages = panel_stages(n_col)
    if carry:
        arrived = swap(parts[0][0], "col", groups)
        piece, lower = add_and_unpack(parts[0][1], arrived, lower, groups)
        arrived = swap(piece, "col", 2 * groups)
        codes.append(add(piece, arrived))
        stages = [[2], [0]]
    for number, bits in enumerate(stages):
        masks = span(bits)[1:]
        period = 1 << min(bits) + len(bits)
        starts = range(0, n_col, period)
        field = period - 1
        if carry and number == 0:
            field = masks[0]
        came = []
        for mask in masks:
            route = [(i, i | mask) for i in starts]
            if carry:
                route = [(i, i ^ mask) for i in range(0, n_col, groups if number == 0 else 1)]
            came.append(lax.ppermute(lower, "col", route))
        if number < len(stages) - 1:
            lower = choose(lower, came, field, masks)
        else:
            message = weigh(lower, came, field, masks, check_weights)
    panel = {}
    came = []
    for mask in span(plans[1][1])[1:]:
        panel[mask] = swap(message, "row", mask)
        came.append(panel[mask])
    message = fold(message, came)
    panel[0] = message
    sums = [message]
    for mask in span(plans[0][1])[1:]:
        panel[mask] = swap(message, "row", mask)
        sums.append(panel[mask])

    results = ()
    for number, (gather, reduce) in enumerate(plans):
        targets = span(reduce)
        lefts = [panel[mask] for mask in targets]
        outs = multiply(span(gather), pivots[None, :], lefts, sums, gathered[number], checks)
        part = dict(zip(targets, outs))
        for place in range(len(reduce) - 1, -1, -1):
            flip = 1 << reduce[place]
            keep = span(reduce[:place])
            sent = [part[mask | flip] for mask in keep]
            message = sent[0] if len(sent) == 1 else jnp.concatenate(sent, axis=0)
            arrived = swap(message, "row", flip)
            if place:
                part = {
                    mask: part[mask] + arrived[i * rows : (i + 1) * rows]
                    for i, mask in enumerate(keep)
                }
        results = subtract(
            number, sides[number], checksum, width, part[0], arrived, results
        )

    for chunk in range(len(codes), len(parts)):
        codes.append(reduce_code(*parts[chunk], groups, position, members))
    parity = ()
    for chunk, piece in enumerate(codes):
        piece, arrived = gather_code(piece, groups, position, members)
        parity = store_code(checkpoints, cuts[chunk], piece, arrived, (rows, cols), parity)
    return (*results, *parity)


def solution(mesh):
    in_specs = (
        P("row", "col"),
        P(),
        P(None, "row"),
        P(None, "col"),
        P("row", "col"),
        P("row", None),
    )
    out_specs = (P("row", "col"), P(None, "col"), P("row", "col"))
    return jax.shard_map(
        per_device, mesh=mesh, in_specs=in_specs, out_specs=out_specs, check_vma=False
    )
```

```python
import jax
import jax.numpy as jnp
from jax import lax
from jax.experimental import pallas as pl
from jax.experimental.pallas import tpu as pltpu
from jax.sharding import PartitionSpec as P


STAGES = ((0, 8, 20, 32, 40), (0, 8, 20, 32, 40), (0, 20, 32, 40))
LANES = 128
GRANT = 8 << 20
ROOM = 67_043_328


VMEM = pl.BlockSpec(memory_space=pltpu.VMEM)
SMEM = pl.BlockSpec(memory_space=pltpu.SMEM)
HBM = pl.BlockSpec(memory_space=pltpu.HBM)


def near(value):
    return pltpu.with_memory_space_constraint(value, pltpu.VMEM)


def swap(value, axis, mask):
    return lax.ppermute(value, axis, [(i, i ^ mask) for i in range(lax.axis_size(axis))])


def span(bits):
    masks = [0]
    for bit in bits:
        masks += [mask | 1 << bit for mask in masks]
    return masks


def bits_of(count):
    return list(range(count.bit_length() - 1))


def plans_of(n_row):
    bits = bits_of(n_row)
    cut = len(bits) // 2
    return [(bits[:cut], bits[cut:]), (bits[cut:], bits[:cut])]


def panel_stages(n_col):
    bits = bits_of(n_col)[1:]
    stages = [bits[i : i + 2] for i in range(0, len(bits), 2)]
    return stages[::-1] + [[0]]


def call(
    kernel, shapes, in_specs, operands, scratch=(), places=None, aliases=None, flops=0, grant=GRANT
):
    places = places or [VMEM] * len(shapes)
    outs = [
        pltpu.VMEM(shape, jnp.float32) if place is VMEM else jax.ShapeDtypeStruct(shape, jnp.float32)
        for shape, place in zip(shapes, places)
    ]
    operands = [near(x) if spec is VMEM else x for x, spec in zip(operands, in_specs)]
    return pl.pallas_call(
        kernel,
        out_shape=outs,
        in_specs=in_specs,
        out_specs=places,
        scratch_shapes=list(scratch),
        input_output_aliases=aliases or {},
        compiler_params=pltpu.CompilerParams(vmem_limit_bytes=grant),
        cost_estimate=pl.CostEstimate(flops=flops, bytes_accessed=0, transcendentals=0),
    )(*operands)


def prepare(matrix, scale, groups, cuts, width, carry):
    rows, cols = matrix.shape
    half = cols // 2
    deep = rows // 2
    count = len(cuts) - 1
    pieces = 2
    step = deep // pieces

    def kernel(matrix_ref, scale_ref, *refs):
        sides, panel_ref, parts, sems = refs[:2], refs[2], refs[3:-1], refs[-1]
        copies = []
        for piece in range(2 * pieces):
            lines = slice(piece * step, (piece + 1) * step)
            for side in range(2):
                copies.append(
                    pltpu.make_async_copy(
                        matrix_ref.at[lines, side * half : (side + 1) * half],
                        sides[side].at[lines, :],
                        sems.at[piece, side],
                    )
                )
        for copy in copies:
            copy.start()
        scale = scale_ref[0, 0]
        upper = lax.axis_index("col") // groups & 1
        for copy in copies:
            copy.wait()
        for number in range(count):
            for side in range(2):
                low = max(cuts[number], side * half)
                high = min(cuts[number + 1], (side + 1) * half)
                if low < high:
                    here = slice(low - side * half, high - side * half)
                    there = slice(low - cuts[number], high - cuts[number])
                    for part in range(2):
                        other = 1 - upper if part == 0 else upper
                        start = pl.multiple_of(deep * other, 8)
                        parts[2 * number + part][:, there] = (
                            sides[side][pl.ds(start, deep), here] * scale
                        )
        panel_ref[...] = sides[0][:, :width]
        if carry:
            for k in range(2):
                there = slice(cuts[1] + k * width, cuts[1] + (k + 1) * width)
                parts[0][:, there] = sides[0][k * deep : (k + 1) * deep, :width]

    shapes = [(rows, half)] * 2 + [(rows, width)]
    for number in range(count):
        size = cuts[number + 1] - cuts[number]
        shapes += [(deep, size + (2 * width if carry and number == 0 else 0)), (deep, size)]
    outs = call(
        kernel,
        shapes,
        [HBM, SMEM],
        [matrix, scale],
        scratch=[pltpu.SemaphoreType.DMA((2 * pieces, 2))],
        grant=ROOM - 4 * (2 * rows * cols + 2 * rows * width) - (1 << 19),
    )
    parts = [(outs[3 + 2 * i], outs[4 + 2 * i]) for i in range(count)]
    return outs[:2], outs[2], parts


def choose(held, arrived, field, masks):
    def kernel(held_ref, *refs):
        digit = lax.axis_index("col") & field
        value = held_ref[...]
        for mask, ref in zip(masks, refs[:-1]):
            value = jnp.where(digit == mask, ref[...], value)
        refs[-1][...] = value

    specs = [VMEM] * (1 + len(arrived))
    return call(kernel, [held.shape], specs, [held, *arrived])[0]


def weigh(held, arrived, field, masks, check_weights):
    rows, width = held.shape
    checks = check_weights.shape[0]

    def kernel(weights_ref, held_ref, *refs):
        digit = lax.axis_index("col") & field
        value = held_ref[...]
        for mask, ref in zip(masks, refs[:-1]):
            value = jnp.where(digit == mask, ref[...], value)
        out_ref = refs[-1]
        out_ref[:rows] = value
        w1, w2, w3 = split(weights_ref[...], 3)
        p1, p2, p3 = split(value, 3)
        left = jnp.concatenate([w1, w1, w2, w2, w1, w3], axis=1)
        right = jnp.concatenate([p1, p2, p1, p2, p3, p1], axis=0)
        out_ref[rows:] = jnp.zeros((8, width), jnp.float32)
        out_ref[rows : rows + checks] = jnp.dot(left, right, preferred_element_type=jnp.float32)

    specs = [VMEM] * (2 + len(arrived))
    operands = [check_weights, held, *arrived]
    return call(kernel, [(rows + 8, width)], specs, operands)[0]


def fold(message, arrived):
    rows = message.shape[0] - 8

    def kernel(message_ref, *refs):
        refs[-1][:rows] = message_ref[:rows]
        total = message_ref[rows:]
        for ref in refs[:-1]:
            total = total + ref[rows:]
        refs[-1][rows:] = total

    return call(kernel, [message.shape], [VMEM] * (1 + len(arrived)), [message, *arrived])[0]


def add(a, b):
    def kernel(a_ref, b_ref, out_ref):
        out_ref[...] = a_ref[...] + b_ref[...]

    return call(kernel, [a.shape], [VMEM, VMEM], [a, b])[0]


def add_and_cut(kept, arrived, cuts, panel, groups):
    height, cols = kept.shape
    count = len(cuts) - 1
    held = [] if panel is None else [panel]

    def kernel(kept_ref, arrived_ref, *refs):
        out_refs = refs[len(held) :]
        for low, high, out_ref in zip(cuts, cuts[1:], out_refs):
            out_ref[...] = kept_ref[:, low:high] + arrived_ref[:, low:high]
        if held:
            rows, width = refs[0].shape
            came = lax.axis_index("col") // groups & 1 == 1
            for k in range(rows // height):
                lines = slice(k * height, (k + 1) * height)
                there = slice(cols + k * width, cols + (k + 1) * width)
                out_refs[count][lines, :] = jnp.where(came, arrived_ref[:, there], refs[0][lines, :])

    shapes = [(height, high - low) for low, high in zip(cuts, cuts[1:])]
    shapes += [panel.shape for panel in held]
    return call(kernel, shapes, [VMEM] * (2 + len(held)), [kept, arrived, *held])


def add_and_join(pairs):
    height = pairs[0][0].shape[0]
    widths = [a.shape[1] for a, _ in pairs]

    def kernel(*refs):
        low = 0
        for k, width in enumerate(widths):
            refs[-1][:, low : low + width] = refs[2 * k][...] + refs[2 * k + 1][...]
            low += width

    operands = [value for pair in pairs for value in pair]
    return call(kernel, [(height, sum(widths))], [VMEM] * len(operands), operands)[0]


def split(value, terms):
    pieces = []
    for _ in range(terms):
        piece = value.astype(jnp.bfloat16)
        value = value - piece.astype(jnp.float32)
        pieces.append(piece)
    return pieces


def multiply(masks, pivots, lefts, sums, blocks, checks):
    width = pivots.shape[1]
    rows, half = blocks[0].shape
    targets = len(lefts)
    depth = len(blocks) * rows
    step = half // max(1, half // 640)

    def kernel(pivots_ref, *refs):
        left_refs, refs = refs[:targets], refs[targets:]
        sum_refs, refs = refs[: len(sums)], refs[len(sums) :]
        block_refs, out_refs = refs[: len(blocks)], refs[len(blocks) :]
        row = lax.broadcasted_iota(jnp.int32, (rows, width), 0)
        own = lax.axis_index("row")
        selector = jnp.concatenate(
            [
                jnp.where(pivots_ref[...] == row + (own ^ mask) * rows, 1.0, 0.0)
                for mask in masks
            ],
            axis=0,
        ).astype(jnp.bfloat16)
        total = sum_refs[0][rows:]
        for ref in sum_refs[1:]:
            total = total + ref[rows:]
        stack = jnp.concatenate([ref[:rows] for ref in left_refs] + [total], axis=0)
        l1, l2 = [
            lax.dot_general(
                piece, selector, (((1,), (1,)), ((), ())), preferred_element_type=jnp.float32
            ).astype(jnp.bfloat16)
            for piece in split(stack, 2)
        ]
        left = jnp.concatenate([l1, l1, l2], axis=1)
        for out_ref in out_refs:
            out_ref[:, half:] = jnp.zeros((rows, LANES), jnp.float32)
        for low in range(0, half, step):
            there = slice(low, low + step)
            x1, x2 = split(jnp.concatenate([ref[:, there] for ref in block_refs], axis=0), 2)
            right = jnp.concatenate([x1, x2, x1], axis=0)
            product = jnp.dot(left, right, preferred_element_type=jnp.float32)
            for k, out_ref in enumerate(out_refs):
                out_ref[:, there] = product[k * rows : (k + 1) * rows]
                for at in range(0, step, LANES):
                    row = (low + at) // LANES * checks
                    out_ref[row : row + checks, half:] = product[
                        targets * rows : targets * rows + checks, at : at + LANES
                    ]

    return call(
        kernel,
        [(rows, half + LANES)] * targets,
        [VMEM] * (1 + targets + len(sums) + len(blocks)),
        [pivots, *lefts, *sums, *blocks],
        flops=2 * (targets * rows + 8) * depth * half,
    )


def subtract(number, matrix, checksum, width, kept, arrived, before):
    rows, half = matrix.shape
    checks, cols = checksum.shape
    pieces = 4

    def kernel(matrix_ref, checksum_ref, kept_ref, arrived_ref, *refs):
        updated_ref, sums_ref, block, line, sems = refs[-5:]
        there = slice(number * half, (number + 1) * half)
        lane = lax.broadcasted_iota(jnp.int32, (1, half), 1)
        live = lane + (lax.axis_index("col") * cols + number * half) >= width
        copies = []
        for k in range(pieces):
            low, high = k * rows // pieces, (k + 1) * rows // pieces
            product = kept_ref[low:high, :half] + arrived_ref[low:high, :half]
            block[low:high, :] = matrix_ref[low:high, :] - jnp.where(live, product, 0.0)
            copies.append(
                pltpu.make_async_copy(
                    block.at[low:high, :], updated_ref.at[low:high, there], sems.at[k]
                )
            )
            copies[-1].start()
        total = kept_ref[:, half:] + arrived_ref[:, half:]
        for at in range(0, half, LANES):
            row = at // LANES * checks
            line[:, at : at + LANES] = checksum_ref[
                :, number * half + at : number * half + at + LANES
            ] - jnp.where(live[:, at : at + LANES], total[row : row + checks], 0.0)
        copies.append(pltpu.make_async_copy(line, sums_ref.at[:, there], sems.at[pieces]))
        copies[-1].start()
        for copy in copies:
            copy.wait()

    return call(
        kernel,
        [(rows, cols), (checks, cols)],
        [VMEM] * 4 + [HBM] * len(before),
        [matrix, checksum, kept, arrived, *before],
        scratch=[
            pltpu.VMEM((rows, half), jnp.float32),
            pltpu.VMEM((checks, half), jnp.float32),
            pltpu.SemaphoreType.DMA((pieces + 1,)),
        ],
        places=[HBM, HBM],
        aliases={4 + i: i for i in range(len(before))},
    )


def store_code(checkpoints, low, piece, arrived, shape, before):
    size, cols = piece.shape
    groups = checkpoints.shape[1]

    def kernel(points_ref, piece_ref, arrived_ref, *refs):
        out_ref, block, sems = refs[-3:]
        index = lax.axis_index("col")
        position = index // groups
        keeper = points_ref[0, 0]
        for k in range(1, groups):
            keeper = jnp.where(index % groups == k, points_ref[0, k], keeper)
        keep = position == keeper
        upper = position & 1 == 1
        copies = []
        for k in range(2):
            there = slice(k * size, (k + 1) * size)
            mine = upper if k else jnp.logical_not(upper)
            value = jnp.where(mine, piece_ref[...], arrived_ref[...])
            block[there, :] = jnp.where(keep, value, 0.0)
            copies.append(
                pltpu.make_async_copy(
                    block.at[there, :],
                    out_ref.at[there, low : low + cols],
                    sems.at[k],
                )
            )
            copies[-1].start()
        for copy in copies:
            copy.wait()

    return call(
        kernel,
        [shape],
        [SMEM] + [VMEM] * 2 + [HBM] * len(before),
        [checkpoints, piece, arrived, *before],
        scratch=[
            pltpu.VMEM((2 * size, cols), jnp.float32),
            pltpu.SemaphoreType.DMA((2,)),
        ],
        places=[HBM],
        aliases={3 + i: i for i in range(len(before))},
    )


def halves(own, upper):
    half = own.shape[0] // 2
    first, second = own[:half], own[half:]
    return jnp.where(upper, first, second), jnp.where(upper, second, first)


def reduce_code(outgoing, kept, stride, position, count):
    bits = bits_of(count)
    for bit in bits[:-1]:
        arrived = swap(outgoing, "col", stride << bit)
        piece = add(kept, arrived)
        if bit + 2 < len(bits):
            outgoing, kept = halves(piece, position >> (bit + 1) & 1 == 1)
    for bit in bits[-1:]:
        arrived = swap(piece, "col", stride << bit)
        piece = add(piece, arrived)
    return piece


def gather_code(piece, stride, position, count):
    bits = bits_of(count)
    for bit in reversed(bits[:-1]):
        arrived = swap(piece, "col", stride << bit)
        if bit == 0:
            return piece, arrived
        upper = position >> bit & 1 == 1
        piece = jnp.concatenate(
            [jnp.where(upper, arrived, piece), jnp.where(upper, piece, arrived)], axis=0
        )


def per_device(matrix, pivots, check_weights, checksum, coefficients, checkpoints):
    rows, cols = matrix.shape
    width = pivots.shape[0]
    checks = check_weights.shape[0]
    col_index = lax.axis_index("col")
    n_row = lax.axis_size("row")
    n_col = lax.axis_size("col")
    groups = checkpoints.shape[1]
    plans = plans_of(n_row)

    position = col_index // groups
    stage_cuts = [
        [cut * (cols // LANES) // ends[-1] * LANES for cut in ends] for ends in STAGES
    ]
    members = n_col // groups
    carry = len(bits_of(members)) == 2 and groups == 2
    cuts = stage_cuts[0]
    sides, lower, parts = prepare(matrix, coefficients, groups, cuts, width, carry)

    gathered = []
    for number, (gather, _) in enumerate(plans):
        blocks = [sides[number]]
        for bit in gather:
            message = blocks[0] if len(blocks) == 1 else jnp.concatenate(blocks, axis=0)
            arrived = swap(message, "row", 1 << bit)
            if len(blocks) == 1:
                blocks.append(arrived)
            else:
                blocks += [arrived[i * rows : (i + 1) * rows] for i in range(len(blocks))]
        gathered.append(blocks)

    stages = panel_stages(n_col)
    firsts = []
    if carry:
        arrived = swap(parts[0][0], "col", groups)
        inside = [cut for cut in stage_cuts[1] if cut <= cuts[1]]
        *firsts, lower = add_and_cut(parts[0][1], arrived, inside, lower, groups)
        stages = [[2], [0]]
    for number, bits in enumerate(stages):
        masks = span(bits)[1:]
        period = 1 << min(bits) + len(bits)
        starts = range(0, n_col, period)
        field = period - 1
        if carry and number == 0:
            field = masks[0]
        came = []
        for mask in masks:
            route = [(i, i | mask) for i in starts]
            if carry:
                route = [(i, i ^ mask) for i in range(0, n_col, groups if number == 0 else 1)]
            came.append(lax.ppermute(lower, "col", route))
        if number < len(stages) - 1:
            lower = choose(lower, came, field, masks)
        else:
            message = weigh(lower, came, field, masks, check_weights)
    panel = {}
    came = []
    for mask in span(plans[1][1])[1:]:
        panel[mask] = swap(message, "row", mask)
        came.append(panel[mask])
    message = fold(message, came)
    panel[0] = message
    sums = [message]
    for mask in span(plans[0][1])[1:]:
        panel[mask] = swap(message, "row", mask)
        sums.append(panel[mask])

    results = ()
    for number, (gather, reduce) in enumerate(plans):
        targets = span(reduce)
        lefts = [panel[mask] for mask in targets]
        outs = multiply(span(gather), pivots[None, :], lefts, sums, gathered[number], checks)
        part = dict(zip(targets, outs))
        for place in range(len(reduce) - 1, -1, -1):
            flip = 1 << reduce[place]
            keep = span(reduce[:place])
            sent = [part[mask | flip] for mask in keep]
            message = sent[0] if len(sent) == 1 else jnp.concatenate(sent, axis=0)
            arrived = swap(message, "row", flip)
            if place:
                part = {
                    mask: part[mask] + arrived[i * rows : (i + 1) * rows]
                    for i, mask in enumerate(keep)
                }
        results = subtract(
            number, sides[number], checksum, width, part[0], arrived, results
        )

    finals = []
    if carry:
        for k in range(1, len(parts)):
            low, high = cuts[k], cuts[k + 1]
            arrived = swap(parts[k][0], "col", groups)
            inside = [cut - low for cut in stage_cuts[1] if low <= cut <= high]
            firsts += add_and_cut(parts[k][1], arrived, inside, None, groups)
        pairs = [(a, swap(a, "col", 2 * groups)) for a in firsts]
        cuts = stage_cuts[2]
        for low, high in zip(cuts, cuts[1:]):
            mine = [pairs[j] for j, cut in enumerate(stage_cuts[1][:-1]) if low <= cut < high]
            piece = add_and_join(mine)
            finals.append((piece, swap(piece, "col", groups)))
    else:
        for part in parts:
            piece = reduce_code(*part, groups, position, members)
            finals.append(gather_code(piece, groups, position, members))
    parity = ()
    for k, (piece, arrived) in enumerate(finals):
        parity = store_code(checkpoints, cuts[k], piece, arrived, (rows, cols), parity)
    return (*results, *parity)


def solution(mesh):
    in_specs = (
        P("row", "col"),
        P(),
        P(None, "row"),
        P(None, "col"),
        P("row", "col"),
        P("row", None),
    )
    out_specs = (P("row", "col"), P(None, "col"), P("row", "col"))
    return jax.shard_map(
        per_device, mesh=mesh, in_specs=in_specs, out_specs=out_specs, check_vma=False
    )
```

```python
import jax
import jax.numpy as jnp
from jax import lax
from jax.experimental import pallas as pl
from jax.experimental.pallas import tpu as pltpu
from jax.sharding import PartitionSpec as P


STAGES = ((0, 8, 20, 32, 40), (0, 8, 20, 32, 40), (0, 20, 32, 40))
LANES = 128
GRANT = 8 << 20
ROOM = 67_043_328


VMEM = pl.BlockSpec(memory_space=pltpu.VMEM)
SMEM = pl.BlockSpec(memory_space=pltpu.SMEM)
HBM = pl.BlockSpec(memory_space=pltpu.HBM)


def near(value):
    return pltpu.with_memory_space_constraint(value, pltpu.VMEM)


def swap(value, axis, mask):
    return lax.ppermute(value, axis, [(i, i ^ mask) for i in range(lax.axis_size(axis))])


def span(bits):
    masks = [0]
    for bit in bits:
        masks += [mask | 1 << bit for mask in masks]
    return masks


def bits_of(count):
    return list(range(count.bit_length() - 1))


def plans_of(n_row):
    bits = bits_of(n_row)
    cut = len(bits) // 2
    return [(bits[:cut], bits[cut:]), (bits[cut:], bits[:cut])]


def panel_stages(n_col):
    bits = bits_of(n_col)[1:]
    stages = [bits[i : i + 2] for i in range(0, len(bits), 2)]
    return stages[::-1] + [[0]]


def call(
    kernel, shapes, in_specs, operands, scratch=(), places=None, aliases=None, flops=0, grant=GRANT
):
    places = places or [VMEM] * len(shapes)
    outs = [
        pltpu.VMEM(shape, jnp.float32) if place is VMEM else jax.ShapeDtypeStruct(shape, jnp.float32)
        for shape, place in zip(shapes, places)
    ]
    operands = [near(x) if spec is VMEM else x for x, spec in zip(operands, in_specs)]
    return pl.pallas_call(
        kernel,
        out_shape=outs,
        in_specs=in_specs,
        out_specs=places,
        scratch_shapes=list(scratch),
        input_output_aliases=aliases or {},
        compiler_params=pltpu.CompilerParams(vmem_limit_bytes=grant),
        cost_estimate=pl.CostEstimate(flops=flops, bytes_accessed=0, transcendentals=0),
    )(*operands)


def prepare(matrix, scale, groups, cuts, width, carry):
    rows, cols = matrix.shape
    half = cols // 2
    deep = rows // 2
    count = len(cuts) - 1
    pieces = 1
    step = deep // pieces

    def kernel(matrix_ref, scale_ref, *refs):
        sides, panel_ref, parts, sems = refs[:2], refs[2], refs[3:-1], refs[-1]
        copies = []
        for piece in range(2 * pieces):
            lines = slice(piece * step, (piece + 1) * step)
            for side in range(2):
                copies.append(
                    pltpu.make_async_copy(
                        matrix_ref.at[lines, side * half : (side + 1) * half],
                        sides[side].at[lines, :],
                        sems.at[piece, side],
                    )
                )
        for copy in copies:
            copy.start()
        scale = scale_ref[0, 0]
        upper = lax.axis_index("col") // groups & 1
        for side in range(2):
            for piece in range(2 * pieces):
                copies[2 * piece + side].wait()
            for number in range(count):
                low = max(cuts[number], side * half)
                high = min(cuts[number + 1], (side + 1) * half)
                if low < high:
                    here = slice(low - side * half, high - side * half)
                    there = slice(low - cuts[number], high - cuts[number])
                    for part in range(2):
                        other = 1 - upper if part == 0 else upper
                        start = pl.multiple_of(deep * other, 8)
                        parts[2 * number + part][:, there] = (
                            sides[side][pl.ds(start, deep), here] * scale
                        )
        panel_ref[...] = sides[0][:, :width]
        if carry:
            for k in range(2):
                there = slice(cuts[1] + k * width, cuts[1] + (k + 1) * width)
                parts[0][:, there] = sides[0][k * deep : (k + 1) * deep, :width]

    shapes = [(rows, half)] * 2 + [(rows, width)]
    for number in range(count):
        size = cuts[number + 1] - cuts[number]
        shapes += [(deep, size + (2 * width if carry and number == 0 else 0)), (deep, size)]
    outs = call(
        kernel,
        shapes,
        [HBM, SMEM],
        [matrix, scale],
        scratch=[pltpu.SemaphoreType.DMA((2 * pieces, 2))],
        grant=ROOM - 4 * (2 * rows * cols + 2 * rows * width) - (1 << 19),
    )
    parts = [(outs[3 + 2 * i], outs[4 + 2 * i]) for i in range(count)]
    return outs[:2], outs[2], parts


def choose(held, arrived, field, masks):
    def kernel(held_ref, *refs):
        digit = lax.axis_index("col") & field
        value = held_ref[...]
        for mask, ref in zip(masks, refs[:-1]):
            value = jnp.where(digit == mask, ref[...], value)
        refs[-1][...] = value

    specs = [VMEM] * (1 + len(arrived))
    return call(kernel, [held.shape], specs, [held, *arrived])[0]


def weigh(held, arrived, field, masks, check_weights):
    rows, width = held.shape
    checks = check_weights.shape[0]

    def kernel(weights_ref, held_ref, *refs):
        digit = lax.axis_index("col") & field
        value = held_ref[...]
        for mask, ref in zip(masks, refs[:-1]):
            value = jnp.where(digit == mask, ref[...], value)
        out_ref = refs[-1]
        out_ref[:rows] = value
        w1, w2, w3 = split(weights_ref[...], 3)
        p1, p2, p3 = split(value, 3)
        left = jnp.concatenate([w1, w1, w2, w2, w1, w3], axis=1)
        right = jnp.concatenate([p1, p2, p1, p2, p3, p1], axis=0)
        out_ref[rows:] = jnp.zeros((8, width), jnp.float32)
        out_ref[rows : rows + checks] = jnp.dot(left, right, preferred_element_type=jnp.float32)

    specs = [VMEM] * (2 + len(arrived))
    operands = [check_weights, held, *arrived]
    return call(kernel, [(rows + 8, width)], specs, operands)[0]


def fold(message, arrived):
    rows = message.shape[0] - 8

    def kernel(message_ref, *refs):
        refs[-1][:rows] = message_ref[:rows]
        total = message_ref[rows:]
        for ref in refs[:-1]:
            total = total + ref[rows:]
        refs[-1][rows:] = total

    return call(kernel, [message.shape], [VMEM] * (1 + len(arrived)), [message, *arrived])[0]


def add(a, b):
    def kernel(a_ref, b_ref, out_ref):
        out_ref[...] = a_ref[...] + b_ref[...]

    return call(kernel, [a.shape], [VMEM, VMEM], [a, b])[0]


def add_and_cut(kept, arrived, cuts, panel, groups):
    height, cols = kept.shape
    count = len(cuts) - 1
    held = [] if panel is None else [panel]

    def kernel(kept_ref, arrived_ref, *refs):
        out_refs = refs[len(held) :]
        for low, high, out_ref in zip(cuts, cuts[1:], out_refs):
            out_ref[...] = kept_ref[:, low:high] + arrived_ref[:, low:high]
        if held:
            rows, width = refs[0].shape
            came = lax.axis_index("col") // groups & 1 == 1
            for k in range(rows // height):
                lines = slice(k * height, (k + 1) * height)
                there = slice(cols + k * width, cols + (k + 1) * width)
                out_refs[count][lines, :] = jnp.where(came, arrived_ref[:, there], refs[0][lines, :])

    shapes = [(height, high - low) for low, high in zip(cuts, cuts[1:])]
    shapes += [panel.shape for panel in held]
    return call(kernel, shapes, [VMEM] * (2 + len(held)), [kept, arrived, *held])


def add_and_join(pairs):
    height = pairs[0][0].shape[0]
    widths = [a.shape[1] for a, _ in pairs]

    def kernel(*refs):
        low = 0
        for k, width in enumerate(widths):
            refs[-1][:, low : low + width] = refs[2 * k][...] + refs[2 * k + 1][...]
            low += width

    operands = [value for pair in pairs for value in pair]
    return call(kernel, [(height, sum(widths))], [VMEM] * len(operands), operands)[0]


def split(value, terms):
    pieces = []
    for _ in range(terms):
        piece = value.astype(jnp.bfloat16)
        value = value - piece.astype(jnp.float32)
        pieces.append(piece)
    return pieces


def multiply(masks, pivots, lefts, sums, blocks, checks):
    width = pivots.shape[1]
    rows, half = blocks[0].shape
    targets = len(lefts)
    depth = len(blocks) * rows
    step = half // max(1, half // 640)

    def kernel(pivots_ref, *refs):
        left_refs, refs = refs[:targets], refs[targets:]
        sum_refs, refs = refs[: len(sums)], refs[len(sums) :]
        block_refs, out_refs = refs[: len(blocks)], refs[len(blocks) :]
        row = lax.broadcasted_iota(jnp.int32, (rows, width), 0)
        own = lax.axis_index("row")
        selector = jnp.concatenate(
            [
                jnp.where(pivots_ref[...] == row + (own ^ mask) * rows, 1.0, 0.0)
                for mask in masks
            ],
            axis=0,
        ).astype(jnp.bfloat16)
        total = sum_refs[0][rows:]
        for ref in sum_refs[1:]:
            total = total + ref[rows:]
        stack = jnp.concatenate([ref[:rows] for ref in left_refs] + [total], axis=0)
        l1, l2 = [
            lax.dot_general(
                piece, selector, (((1,), (1,)), ((), ())), preferred_element_type=jnp.float32
            ).astype(jnp.bfloat16)
            for piece in split(stack, 2)
        ]
        left = jnp.concatenate([l1, l1, l2], axis=1)
        for out_ref in out_refs:
            out_ref[:, half:] = jnp.zeros((rows, LANES), jnp.float32)
        for low in range(0, half, step):
            there = slice(low, low + step)
            x1, x2 = split(jnp.concatenate([ref[:, there] for ref in block_refs], axis=0), 2)
            right = jnp.concatenate([x1, x2, x1], axis=0)
            product = jnp.dot(left, right, preferred_element_type=jnp.float32)
            for k, out_ref in enumerate(out_refs):
                out_ref[:, there] = product[k * rows : (k + 1) * rows]
                for at in range(0, step, LANES):
                    row = (low + at) // LANES * checks
                    out_ref[row : row + checks, half:] = product[
                        targets * rows : targets * rows + checks, at : at + LANES
                    ]

    return call(
        kernel,
        [(rows, half + LANES)] * targets,
        [VMEM] * (1 + targets + len(sums) + len(blocks)),
        [pivots, *lefts, *sums, *blocks],
        flops=2 * (targets * rows + 8) * depth * half,
    )


def subtract(number, matrix, checksum, width, kept, arrived, before):
    rows, half = matrix.shape
    checks, cols = checksum.shape
    pieces = 4

    def kernel(matrix_ref, checksum_ref, kept_ref, arrived_ref, *refs):
        updated_ref, sums_ref, block, line, sems = refs[-5:]
        there = slice(number * half, (number + 1) * half)
        lane = lax.broadcasted_iota(jnp.int32, (1, half), 1)
        live = lane + (lax.axis_index("col") * cols + number * half) >= width
        copies = []
        for k in range(pieces):
            low, high = k * rows // pieces, (k + 1) * rows // pieces
            product = kept_ref[low:high, :half] + arrived_ref[low:high, :half]
            block[low:high, :] = matrix_ref[low:high, :] - jnp.where(live, product, 0.0)
            copies.append(
                pltpu.make_async_copy(
                    block.at[low:high, :], updated_ref.at[low:high, there], sems.at[k]
                )
            )
            copies[-1].start()
        total = kept_ref[:, half:] + arrived_ref[:, half:]
        for at in range(0, half, LANES):
            row = at // LANES * checks
            line[:, at : at + LANES] = checksum_ref[
                :, number * half + at : number * half + at + LANES
            ] - jnp.where(live[:, at : at + LANES], total[row : row + checks], 0.0)
        copies.append(pltpu.make_async_copy(line, sums_ref.at[:, there], sems.at[pieces]))
        copies[-1].start()
        for copy in copies:
            copy.wait()

    return call(
        kernel,
        [(rows, cols), (checks, cols)],
        [VMEM] * 4 + [HBM] * len(before),
        [matrix, checksum, kept, arrived, *before],
        scratch=[
            pltpu.VMEM((rows, half), jnp.float32),
            pltpu.VMEM((checks, half), jnp.float32),
            pltpu.SemaphoreType.DMA((pieces + 1,)),
        ],
        places=[HBM, HBM],
        aliases={4 + i: i for i in range(len(before))},
    )


def store_code(checkpoints, low, piece, arrived, shape, before):
    size, cols = piece.shape
    groups = checkpoints.shape[1]

    def kernel(points_ref, piece_ref, arrived_ref, *refs):
        out_ref, block, sems = refs[-3:]
        index = lax.axis_index("col")
        position = index // groups
        keeper = points_ref[0, 0]
        for k in range(1, groups):
            keeper = jnp.where(index % groups == k, points_ref[0, k], keeper)
        keep = position == keeper
        upper = position & 1 == 1
        copies = []
        for k in range(2):
            there = slice(k * size, (k + 1) * size)
            mine = upper if k else jnp.logical_not(upper)
            value = jnp.where(mine, piece_ref[...], arrived_ref[...])
            block[there, :] = jnp.where(keep, value, 0.0)
            copies.append(
                pltpu.make_async_copy(
                    block.at[there, :],
                    out_ref.at[there, low : low + cols],
                    sems.at[k],
                )
            )
            copies[-1].start()
        for copy in copies:
            copy.wait()

    return call(
        kernel,
        [shape],
        [SMEM] + [VMEM] * 2 + [HBM] * len(before),
        [checkpoints, piece, arrived, *before],
        scratch=[
            pltpu.VMEM((2 * size, cols), jnp.float32),
            pltpu.SemaphoreType.DMA((2,)),
        ],
        places=[HBM],
        aliases={3 + i: i for i in range(len(before))},
    )


def halves(own, upper):
    half = own.shape[0] // 2
    first, second = own[:half], own[half:]
    return jnp.where(upper, first, second), jnp.where(upper, second, first)


def reduce_code(outgoing, kept, stride, position, count):
    bits = bits_of(count)
    for bit in bits[:-1]:
        arrived = swap(outgoing, "col", stride << bit)
        piece = add(kept, arrived)
        if bit + 2 < len(bits):
            outgoing, kept = halves(piece, position >> (bit + 1) & 1 == 1)
    for bit in bits[-1:]:
        arrived = swap(piece, "col", stride << bit)
        piece = add(piece, arrived)
    return piece


def gather_code(piece, stride, position, count):
    bits = bits_of(count)
    for bit in reversed(bits[:-1]):
        arrived = swap(piece, "col", stride << bit)
        if bit == 0:
            return piece, arrived
        upper = position >> bit & 1 == 1
        piece = jnp.concatenate(
            [jnp.where(upper, arrived, piece), jnp.where(upper, piece, arrived)], axis=0
        )


def per_device(matrix, pivots, check_weights, checksum, coefficients, checkpoints):
    rows, cols = matrix.shape
    width = pivots.shape[0]
    checks = check_weights.shape[0]
    col_index = lax.axis_index("col")
    n_row = lax.axis_size("row")
    n_col = lax.axis_size("col")
    groups = checkpoints.shape[1]
    plans = plans_of(n_row)

    position = col_index // groups
    stage_cuts = [
        [cut * (cols // LANES) // ends[-1] * LANES for cut in ends] for ends in STAGES
    ]
    members = n_col // groups
    carry = len(bits_of(members)) == 2 and groups == 2
    cuts = stage_cuts[0]
    sides, lower, parts = prepare(matrix, coefficients, groups, cuts, width, carry)

    gathered = []
    for number, (gather, _) in enumerate(plans):
        blocks = [sides[number]]
        for bit in gather:
            message = blocks[0] if len(blocks) == 1 else jnp.concatenate(blocks, axis=0)
            arrived = swap(message, "row", 1 << bit)
            if len(blocks) == 1:
                blocks.append(arrived)
            else:
                blocks += [arrived[i * rows : (i + 1) * rows] for i in range(len(blocks))]
        gathered.append(blocks)

    stages = panel_stages(n_col)
    firsts = []
    if carry:
        arrived = swap(parts[0][0], "col", groups)
        inside = [cut for cut in stage_cuts[1] if cut <= cuts[1]]
        *firsts, lower = add_and_cut(parts[0][1], arrived, inside, lower, groups)
        stages = [[2], [0]]
    for number, bits in enumerate(stages):
        masks = span(bits)[1:]
        period = 1 << min(bits) + len(bits)
        starts = range(0, n_col, period)
        field = period - 1
        if carry and number == 0:
            field = masks[0]
        came = []
        for mask in masks:
            route = [(i, i | mask) for i in starts]
            if carry:
                route = [(i, i ^ mask) for i in range(0, n_col, groups if number == 0 else 1)]
            came.append(lax.ppermute(lower, "col", route))
        if number < len(stages) - 1:
            lower = choose(lower, came, field, masks)
        else:
            message = weigh(lower, came, field, masks, check_weights)
    panel = {}
    came = []
    for mask in span(plans[1][1])[1:]:
        panel[mask] = swap(message, "row", mask)
        came.append(panel[mask])
    message = fold(message, came)
    panel[0] = message
    sums = [message]
    for mask in span(plans[0][1])[1:]:
        panel[mask] = swap(message, "row", mask)
        sums.append(panel[mask])

    results = ()
    for number, (gather, reduce) in enumerate(plans):
        targets = span(reduce)
        lefts = [panel[mask] for mask in targets]
        outs = multiply(span(gather), pivots[None, :], lefts, sums, gathered[number], checks)
        part = dict(zip(targets, outs))
        for place in range(len(reduce) - 1, -1, -1):
            flip = 1 << reduce[place]
            keep = span(reduce[:place])
            sent = [part[mask | flip] for mask in keep]
            message = sent[0] if len(sent) == 1 else jnp.concatenate(sent, axis=0)
            arrived = swap(message, "row", flip)
            if place:
                part = {
                    mask: part[mask] + arrived[i * rows : (i + 1) * rows]
                    for i, mask in enumerate(keep)
                }
        results = subtract(
            number, sides[number], checksum, width, part[0], arrived, results
        )

    finals = []
    if carry:
        for k in range(1, len(parts)):
            low, high = cuts[k], cuts[k + 1]
            arrived = swap(parts[k][0], "col", groups)
            inside = [cut - low for cut in stage_cuts[1] if low <= cut <= high]
            firsts += add_and_cut(parts[k][1], arrived, inside, None, groups)
        pairs = [(a, swap(a, "col", 2 * groups)) for a in firsts]
        cuts = stage_cuts[2]
        for low, high in zip(cuts, cuts[1:]):
            mine = [pairs[j] for j, cut in enumerate(stage_cuts[1][:-1]) if low <= cut < high]
            piece = add_and_join(mine)
            finals.append((piece, swap(piece, "col", groups)))
    else:
        for part in parts:
            piece = reduce_code(*part, groups, position, members)
            finals.append(gather_code(piece, groups, position, members))
    parity = ()
    for k, (piece, arrived) in enumerate(finals):
        parity = store_code(checkpoints, cuts[k], piece, arrived, (rows, cols), parity)
    return (*results, *parity)


def solution(mesh):
    in_specs = (
        P("row", "col"),
        P(),
        P(None, "row"),
        P(None, "col"),
        P("row", "col"),
        P("row", None),
    )
    out_specs = (P("row", "col"), P(None, "col"), P("row", "col"))
    return jax.shard_map(
        per_device, mesh=mesh, in_specs=in_specs, out_specs=out_specs, check_vma=False
    )
```
